512 devices in a mesh: seq: 64 (over x, y, core), head: 8 (over z).
Axes of the slice: x: 4, y: 8, z: 8, core: 2. Of those that a mesh axis runs over, the one named last changes fastest.
Arguments:
- query_feat: bfloat16 [32768, 512], P('seq', 'head'), may hold values from -6 to 6
- key_feat: bfloat16 [32768, 512], P('seq', 'head'), may hold values from -6 to 6
- values: bfloat16 [32768, 4096], P('seq', 'head'), may hold values from -6 to 6
- conv_query: float32 [3, 512], P(None, 'head'), may hold values from -3 to 3
- conv_key: float32 [3, 512], P(None, 'head'), may hold values from -3 to 3
- conv_value: float32 [3, 4096], P(None, 'head'), may hold values from -3 to 3
- norm_gain: float32 [4096], P('head'), may hold values from 0.1 to 1.9
- out_weight: bfloat16 [4096, 4096], P('head', 'seq'), may hold values from -0.09375 to 0.09375
- stream_ids: int32 [64], replicated, may hold values from 0 to 7, never falling along the last dimension, each value on 1 to 32 neighbouring positions
Outputs:
- mixed: bfloat16 [32768, 4096], P('seq', 'head')
The draws below stay inside these ranges and needn't reach their ends.
Inputs may be any that keep to these rules, and one draw needn't show every extreme that they name: `stream_ids`: stream ids never fall along the shards; each stream holds 1 to 32 consecutive shards, and one stream holds exactly 32.
All inputs are finite; a program needn't handle non-finite values.
Results may differ from the reference program's by a relative error of at most 0.018.
Values may be sent and summed in bfloat16 or wider, within the bound.
A program may use at most 128 MiB of HBM per device.

```python
import math
import jax
import jax.numpy as jnp
import numpy as np
from jax import lax

D = 4096
HEADS = 32
HD = 128
FEAT = 16
TOK_DEV = 512
TAYLOR = 273
BLOCK = 512
TOKENS = 32768
SHARDS = 64
STREAMS = 8
MOST_RUN = 32
N_HEAD = 8


def block_levels(rng, extent, shards, low, largest):
    def one(axis_at, parts):
        heights = jax.random.uniform(jax.random.fold_in(jax.random.fold_in(rng, 6), axis_at), (parts,), jnp.float32, low / len(shards), largest / len(shards))
        return jnp.repeat(jnp.exp(heights), extent[axis_at] // parts).reshape((-1,) + (1,) * (len(extent) - axis_at - 1))

    level = one(*shards[0])
    for cut in shards[1:]:
        level = level * one(*cut)
    return level


def profile(number_of, total, limit, slope):
    portions = [(1 << 20) // math.isqrt(standing ** slope) + 1 for standing in range(2, number_of + 1)]
    spare, holding = total - limit - (number_of - 1), [1] * (number_of - 1)
    while spare > 0:
        candidates = [i for i in range(number_of - 1) if holding[i] < limit]
        pool, left = sum([portions[i] for i in candidates]), spare
        for i in candidates:
            extra = min(limit - holding[i], max(1, left * portions[i] // pool), spare)
            holding[i] = holding[i] + extra
            spare = spare - extra
    return np.array([limit] + holding)


def ragged_sizes(rng, number_of, total, most, skew):
    if number_of == 2:
        one = jax.random.randint(rng, (), max(1, total - most), min(most, total - 1) + 1)
        return jnp.stack([one, total - one])
    sizes = jnp.asarray(profile(number_of, total, most, skew), jnp.int32)
    pairs = (number_of - 1) // 2
    giver, taker = sizes[1:1 + 2 * pairs:2], sizes[2:2 + 2 * pairs:2]
    margin = jnp.minimum(giver - 1, most - taker)
    shifted = jax.random.randint(jax.random.fold_in(rng, 1), (pairs,), 0, 1 << 20) % (margin + 1)
    sizes = sizes.at[1:1 + 2 * pairs:2].set(giver - shifted).at[2:2 + 2 * pairs:2].set(taker + shifted)
    return sizes[jax.random.permutation(jax.random.fold_in(rng, 2), number_of)]


def gaussian(stream_key, extent, scale, reach, pieces=(), kind=jnp.bfloat16):
    array = jax.random.normal(stream_key, extent, jnp.float32) * scale
    if len(pieces) > 0:
        array = block_levels(stream_key, extent, pieces, -0.22, 0.18) * array
    return jnp.clip(array, min=-reach, max=reach).astype(kind)


def setup_inputs(seed: int = 0) -> dict:
    seeds = jax.random.split(jax.random.key(seed), 10)
    return {
        "query_feat": gaussian(seeds[0], (TOKENS, HEADS * FEAT), 1.0, 6.0, ((0, 64), (1, 8))),
        "key_feat": gaussian(seeds[1], (TOKENS, HEADS * FEAT), 1.0, 6.0, ((0, 64), (1, 8))),
        "values": gaussian(seeds[2], (TOKENS, HEADS * HD), 1.0, 6.0, ((0, 64), (1, 8))),
        "conv_query": gaussian(seeds[3], (3, HEADS * FEAT), 0.6, 3.0, ((1, 8),), jnp.float32),
        "conv_key": gaussian(seeds[4], (3, HEADS * FEAT), 0.6, 3.0, ((1, 8),), jnp.float32),
        "conv_value": gaussian(seeds[5], (3, HEADS * HD), 0.6, 3.0, ((1, 8),), jnp.float32),
        "norm_gain": jnp.clip(1.0 + 0.18 * jax.random.normal(seeds[6], (HEADS * HD,), jnp.float32), 0.1, 1.9),
        "out_weight": gaussian(seeds[7], (HEADS * HD, D), (HEADS * HD) ** -0.5, 0.09375, ((0, 8), (1, 64))),
        "stream_ids": jnp.searchsorted(jnp.cumsum(ragged_sizes(seeds[8], STREAMS, SHARDS, MOST_RUN, 2)), jnp.arange(SHARDS), side="right").astype(jnp.int32),
    }


def taylor(feats):
    scaled = feats * FEAT ** (-0.25)
    outer = (scaled[..., :, None] * scaled[..., None, :]).reshape(scaled.shape[:-1] + (FEAT * FEAT,)) * 0.5 ** 0.5
    ones = jnp.ones(scaled.shape[:-1] + (1,), jnp.float32)
    return jnp.concatenate([ones, scaled, outer], axis=-1)

def causal_conv(inputs, kernel, keep_one, keep_two):
    floats = inputs.astype(jnp.float32)
    width = floats.shape[1]
    prev_one = jnp.concatenate([jnp.zeros((1, width), jnp.float32), floats[:-1]], axis=0) * keep_one[:, None]
    prev_two = jnp.concatenate([jnp.zeros((2, width), jnp.float32), floats[:-2]], axis=0) * keep_two[:, None]
    return (kernel[0] * prev_two + kernel[1] * prev_one + kernel[2] * floats).astype(jnp.bfloat16)

def reference(query_feat, key_feat, values, conv_query, conv_key, conv_value, norm_gain, out_weight, stream_ids):
    tokens = query_feat.shape[0]
    shard_start = jnp.concatenate([jnp.ones((1,), jnp.float32), (stream_ids[1:] != stream_ids[:-1]).astype(jnp.float32)])
    positions = jnp.arange(tokens, dtype=jnp.int32)
    row_start = shard_start[positions // TOK_DEV]
    inner = positions % TOK_DEV
    keep_one = 1.0 - row_start * (inner < 1).astype(jnp.float32)
    keep_two = 1.0 - row_start * (inner < 2).astype(jnp.float32)
    qconv = causal_conv(query_feat, conv_query, keep_one, keep_two)
    kconv = causal_conv(key_feat, conv_key, keep_one, keep_two)
    vconv = causal_conv(values, conv_value, keep_one, keep_two)
    nblocks = tokens // BLOCK
    blocks = jnp.arange(nblocks, dtype=jnp.int32)
    first_block = (blocks * BLOCK % TOK_DEV == 0).astype(jnp.float32)
    reset = first_block * shard_start[blocks * BLOCK // TOK_DEV]
    qheads = qconv.reshape(tokens, HEADS, FEAT).transpose(1, 0, 2)
    kheads = kconv.reshape(tokens, HEADS, FEAT).transpose(1, 0, 2)
    vheads = vconv.reshape(tokens, HEADS, HD).transpose(1, 0, 2)
    gains = norm_gain.reshape(HEADS, HD)
    causal = jnp.tril(jnp.ones((BLOCK, BLOCK), jnp.float32))
    high = lax.Precision.HIGHEST

    def one_head(inputs):
        qhead, khead, vhead, gain = inputs
        phq = taylor(qhead.astype(jnp.float32)).astype(jnp.bfloat16).reshape(nblocks, BLOCK, TAYLOR).astype(jnp.float32)
        phk = taylor(khead.astype(jnp.float32)).astype(jnp.bfloat16).reshape(nblocks, BLOCK, TAYLOR).astype(jnp.float32)
        vblock = vhead.reshape(nblocks, BLOCK, HD).astype(jnp.float32)
        scores = jnp.einsum('bif,bjf->bij', phq, phk, precision=high) * causal
        scores = scores.astype(jnp.bfloat16).astype(jnp.float32)
        local = jnp.einsum('bij,bjd->bid', scores, vblock, precision=high)
        kvsum = jnp.einsum('bjf,bjd->bfd', phk, vblock, precision=high)

        def advance(carry, pair):
            block_kv, flag = pair
            entering = carry * (1.0 - flag)
            return (entering + block_kv, entering)
        _, states = lax.scan(advance, jnp.zeros((TAYLOR, HD), jnp.float32), (kvsum, reset))
        carried = jnp.einsum('bif,bfd->bid', phq, states, precision=high)
        result = (local + carried).reshape(tokens, HD)
        normed = result * lax.rsqrt(lax.optimization_barrier(jnp.mean(result * result, axis=-1, keepdims=True)) + 1e-05) * gain
        return normed.astype(jnp.bfloat16)
    hidden = lax.map(one_head, (qheads, kheads, vheads, gains))
    hidden = hidden.transpose(1, 0, 2).reshape(tokens, HEADS * HD)
    group = HEADS * HD // N_HEAD
    total = jnp.zeros((tokens, D), jnp.float32)
    for member in range(N_HEAD):
        partial_sum = jnp.dot(hidden[:, member * group:(member + 1) * group], out_weight[member * group:(member + 1) * group], preferred_element_type=jnp.float32)
        total = total + lax.optimization_barrier(partial_sum.astype(jnp.bfloat16)).astype(jnp.float32)
    return total.astype(jnp.bfloat16)
```

```python
import numpy as np
import jax
import jax.numpy as jnp
from jax import lax
from jax.sharding import PartitionSpec as P

HD = 128
FEAT = 16
PAD = 160


def tables(heads):
    left = np.zeros((heads * FEAT, heads * PAD), np.float32)
    right = np.zeros((heads * FEAT, heads * PAD), np.float32)
    add_left = np.zeros((1, heads * PAD), np.float32)
    add_right = np.zeros((1, heads * PAD), np.float32)
    scale = np.zeros((1, heads * PAD), np.float32)
    twice = np.zeros((1, heads * PAD), np.float32)
    for h in range(heads):
        at = h * PAD
        add_left[0, at] = add_right[0, at] = scale[0, at] = twice[0, at] = 1.0
        for i in range(FEAT):
            at = h * PAD + 1 + i
            left[h * FEAT + i, at] = 1.0
            add_right[0, at] = scale[0, at] = twice[0, at] = 1.0
        at = h * PAD + 1 + FEAT
        for i in range(FEAT):
            for j in range(i, FEAT):
                left[h * FEAT + i, at] = 1.0
                right[h * FEAT + j, at] = 1.0
                scale[0, at] = np.float32(0.5**0.5)
                twice[0, at] = 1.0 if i == j else 2.0
                at += 1
    return left, right, add_left, add_right, scale, twice


def taylor(conv, heads):
    left, right, add_left, add_right, scale, twice = tables(heads)
    a = (conv.astype(jnp.float32) * FEAT ** (-0.25)).astype(jnp.bfloat16)
    one = jnp.dot(a, jnp.asarray(left, jnp.bfloat16), preferred_element_type=jnp.float32) + add_left
    two = jnp.dot(a, jnp.asarray(right, jnp.bfloat16), preferred_element_type=jnp.float32) + add_right
    return ((one * two) * scale).astype(jnp.bfloat16), jnp.asarray(twice, jnp.bfloat16)


def convolve(inputs, rim_rows, kernel, keep):
    padded = jnp.concatenate(
        [rim_rows.astype(jnp.float32) * keep, inputs.astype(jnp.float32)], axis=0
    )
    return (kernel[0] * padded[:-2] + kernel[1] * padded[1:-1] + kernel[2] * padded[2:]).astype(
        jnp.bfloat16
    )


def on_device(
    query_feat,
    key_feat,
    values,
    conv_query,
    conv_key,
    conv_value,
    norm_gain,
    out_weight,
    stream_ids,
):
    rows, qw = query_feat.shape
    heads = values.shape[1] // HD
    shards = lax.axis_size("seq")
    weight = lax.all_gather(out_weight.T, "seq", axis=0, tiled=True)
    position = lax.axis_index("seq")
    own_stream = stream_ids[position]
    prior_stream = stream_ids[jnp.maximum(position - 1, 0)]
    keep = 1.0 - jnp.logical_or(position == 0, own_stream != prior_stream).astype(jnp.float32)
    rim = jnp.concatenate([query_feat[-2:], key_feat[-2:], values[-2:]], axis=1)
    rim = lax.ppermute(rim, "seq", [(i, i + 1) for i in range(shards - 1)])
    qconv = convolve(query_feat, rim[:, :qw], conv_query, keep)
    kconv = convolve(key_feat, rim[:, qw : 2 * qw], conv_key, keep)
    vconv = convolve(values, rim[:, 2 * qw :], conv_value, keep)
    phk, twice = taylor(kconv, heads)
    kv = [
        lax.dot_general(
            phk[:, h * PAD : (h + 1) * PAD],
            vconv[:, h * HD : (h + 1) * HD],
            (((0,), (0,)), ((), ())),
            preferred_element_type=jnp.float32,
        )
        for h in range(heads)
    ]
    pieces = jnp.concatenate(kv, axis=0).astype(jnp.bfloat16).reshape(shards, -1, HD)
    pieces = lax.all_to_all(pieces, "seq", 0, 0, tiled=True)
    order = jnp.arange(shards)
    earlier = (stream_ids[:, None] == stream_ids[None, :]) & (order[None, :] < order[:, None])
    sums = jnp.einsum(
        "ds,skl->dkl", earlier.astype(jnp.bfloat16), pieces, preferred_element_type=jnp.float32
    ).astype(jnp.bfloat16)
    state = lax.all_to_all(sums, "seq", 0, 0, tiled=True).reshape(heads, PAD, HD)
    phq, _ = taylor(qconv, heads)
    phq = phq * twice
    causal = jnp.tril(jnp.ones((rows, rows), jnp.bool_))
    hidden = []
    for h in range(heads):
        q = phq[:, h * PAD : (h + 1) * PAD]
        k = phk[:, h * PAD : (h + 1) * PAD]
        v = vconv[:, h * HD : (h + 1) * HD]
        scores = lax.dot_general(
            q, k, (((1,), (1,)), ((), ())), preferred_element_type=jnp.float32
        )
        scores = jnp.where(causal, scores, 0.0).astype(jnp.bfloat16)
        y = jnp.dot(scores, v, preferred_element_type=jnp.float32) + jnp.dot(
            q, state[h], preferred_element_type=jnp.float32
        )
        gain = norm_gain[h * HD : (h + 1) * HD]
        y = y * lax.rsqrt(jnp.mean(y * y, axis=-1, keepdims=True) + 1e-05) * gain
        hidden.append(y.astype(jnp.bfloat16))
    hidden = jnp.concatenate(hidden, axis=1)
    terms = lax.dot_general(
        hidden, weight, (((1,), (1,)), ((), ())), preferred_element_type=jnp.float32
    )
    return lax.psum_scatter(terms.astype(jnp.bfloat16), "head", scatter_dimension=1, tiled=True)


def solution(mesh):
    placed = (
        P("seq", "head"),
        P("seq", "head"),
        P("seq", "head"),
        P(None, "head"),
        P(None, "head"),
        P(None, "head"),
        P("head"),
        P("head", "seq"),
        P(),
    )
    return jax.shard_map(
        on_device, mesh=mesh, in_specs=placed, out_specs=P("seq", "head"), check_vma=False
    )
```

```python
import numpy as np
import jax
import jax.numpy as jnp
from jax import lax
from jax.experimental import pallas as pl
from jax.experimental.pallas import tpu as pltpu
from jax.sharding import PartitionSpec as P

HD = 128
FEAT = 16
PAD = 160
X, Y, C = 4, 8, 2
SHARDS = X * Y * C
Z = 8
TILE = 16
MESH = pl.DeviceIdType.MESH


def remote(src, dst, send_sem, recv_sem, axis, target):
    return pltpu.make_async_remote_copy(
        src_ref=src,
        dst_ref=dst,
        send_sem=send_sem,
        recv_sem=recv_sem,
        device_id={axis: target},
        device_id_type=MESH,
    )


def exchange_kernel(
    ids,
    pieces,
    w_ref,
    wout,
    state,
    inbox,
    sums,
    own_sem,
    x_send,
    x_recv,
    y_send,
    y_recv,
    c_send,
    c_recv,
    one_send,
    one_recv,
    two_send,
    two_recv,
    local_sem,
):
    npieces = pieces.shape[0]
    me = lax.axis_index("seq")
    c = lax.rem(me, C)
    y = lax.rem(me // C, Y)
    x = me // (C * Y)

    def at(xx, yy, cc):
        return (lax.rem(xx + X, X) * Y + lax.rem(yy + Y, Y)) * C + cc

    barrier = pltpu.get_barrier_semaphore()

    @pl.loop(1, SHARDS)
    def _(j):
        pl.semaphore_signal(
            barrier, inc=1, device_id={"seq": lax.rem(me + j, SHARDS)}, device_id_type=MESH
        )

    own = pltpu.make_async_copy(w_ref, wout.at[x, y, c], own_sem)
    own.start()
    pl.semaphore_wait(barrier, SHARDS - 1)

    along_x = [
        remote(w_ref, wout.at[x, y, c], x_send.at[k], x_recv.at[k], "seq", at(x + k + 1, y, c))
        for k in range(X - 1)
    ]
    for copy in along_x:
        copy.start()

    @pl.loop(0, npieces)
    def _(p):
        @pl.when(p != me)
        def _():
            remote(pieces.at[p], inbox.at[me], one_send, one_recv, "seq", p).start()

    handler = me < npieces

    @pl.when(handler)
    def _():
        keep = pltpu.make_async_copy(pieces.at[me], inbox.at[me], local_sem)
        keep.start()
        keep.wait()

    def group(yy, part=None):
        yy = lax.rem(yy + Y, Y)
        if part is None:
            return wout.at[:, yy, c]
        return wout.at[part * (X // 2) : (part + 1) * (X // 2), yy, c]

    def hop(k, up):
        part = None if k < 3 else (0 if up else 1)
        ref = group(y - k if up else y + k, part)
        return remote(
            ref,
            ref,
            y_send.at[0 if up else 1, k],
            y_recv.at[0 if up else 1, k],
            "seq",
            at(x, y + 1 if up else y - 1, c),
        )

    def across(j, yy):
        ref = group(yy)
        return remote(ref, ref, c_send.at[j], c_recv.at[j], "seq", at(x, y, 1 - c))

    own.wait()
    for copy in along_x:
        copy.wait_recv()
    hops = [(hop(k, True), hop(k, False)) for k in range(4)]
    partner = [across(0, y)]
    for copy in hops[0]:
        copy.start()
    partner[0].start()

    @pl.when(handler)
    def _():
        pltpu.make_async_copy(
            inbox.at[pl.ds(0, SHARDS - 1)], inbox.at[pl.ds(0, SHARDS - 1)], one_recv
        ).wait()

        def step(s, acc):
            before = jnp.maximum(s - 1, 0)
            same = jnp.where((s > 0) & (ids[s] == ids[before]), 1.0, 0.0)
            acc = (acc + inbox[before].astype(jnp.float32)) * same
            sums[s] = acc.astype(jnp.bfloat16)
            return acc

        lax.fori_loop(0, SHARDS, step, jnp.zeros(inbox.shape[1:], jnp.float32))

        @pl.loop(0, SHARDS)
        def _(s):
            @pl.when(s != me)
            def _():
                remote(sums.at[s], state.at[me], two_send, two_recv, "seq", s).start()

        keep = pltpu.make_async_copy(sums.at[me], state.at[me], local_sem)
        keep.start()
        keep.wait()

    for k in range(3):
        hops[k][0].wait_recv()
        hops[k][1].wait_recv()
        for copy in hops[k + 1]:
            copy.start()
        for j, yy in ((1 + 2 * k, y - 1 - k), (2 + 2 * k, y + 1 + k)):
            partner.append(across(j, yy))
            partner[-1].start()
    hops[3][0].wait_recv()
    hops[3][1].wait_recv()
    partner.append(across(7, y + 4))
    partner[-1].start()

    def drain(count, sem):
        pltpu.make_async_copy(
            inbox.at[pl.ds(0, count)], inbox.at[pl.ds(0, count)], sem
        ).wait()

    @pl.when(handler)
    def _():
        drain(npieces - 1, two_recv)
        drain(SHARDS - 1, two_send)
        drain(npieces - 1, one_send)

    @pl.when(jnp.logical_not(handler))
    def _():
        drain(npieces, two_recv)
        drain(npieces, one_send)

    for copy in along_x:
        copy.wait_send()
    for pair in hops:
        for copy in pair:
            copy.wait_send()
    for copy in partner:
        copy.wait()


def exchange(ids, pieces, block):
    dma = pltpu.SemaphoreType.DMA
    vmem = pl.BlockSpec(memory_space=pltpu.VMEM)
    return pl.pallas_call(
        exchange_kernel,
        out_shape=(
            jax.ShapeDtypeStruct((X, Y, C) + block.shape, block.dtype),
            jax.ShapeDtypeStruct(pieces.shape, pieces.dtype),
        ),
        in_specs=[pl.BlockSpec(memory_space=pltpu.SMEM), vmem, vmem],
        out_specs=(vmem, vmem),
        scratch_shapes=[
            pltpu.VMEM((SHARDS,) + pieces.shape[1:], jnp.bfloat16),
            pltpu.VMEM((SHARDS,) + pieces.shape[1:], jnp.bfloat16),
            dma,
            dma((X - 1,)),
            dma((X - 1,)),
            dma((2, 4)),
            dma((2, 4)),
            dma((Y,)),
            dma((Y,)),
            dma,
            dma,
            dma,
            dma,
            dma,
        ],
        compiler_params=pltpu.CompilerParams(
            collective_id=0, has_side_effects=True, vmem_limit_bytes=24 << 20
        ),
    )(ids, pieces, block)


def project_kernel(hidden, weight, out, outbox, inbox, send, recv):
    z = lax.axis_index("head")
    up, down = lax.rem(z + 1, Z), lax.rem(z + Z - 1, Z)
    barrier = pltpu.get_barrier_semaphore()
    for neighbour in (up, down):
        pl.semaphore_signal(barrier, inc=1, device_id={"head": neighbour}, device_id_type=MESH)
    rows, cols = out.shape
    half_rows, half_cols = rows // 2, cols // 2

    def term(k, way, part):
        goal = lax.rem(z + 2 * Z - 1 - k, Z) if way == 0 else lax.rem(z + 1 + k, Z)
        first = pl.multiple_of(goal * cols + way * half_cols, half_cols)
        return lax.dot_general(
            hidden[part * half_rows : (part + 1) * half_rows, :],
            weight[pl.ds(first, half_cols), :],
            (((1,), (1,)), ((), ())),
            preferred_element_type=jnp.float32,
        )

    def copy(k, way, part):
        return remote(
            outbox.at[k, way, part],
            inbox.at[k, way, part],
            send.at[k, way, part],
            recv.at[k, way, part],
            "head",
            up if way == 0 else down,
        )

    streams = [(way, part) for part in range(2) for way in range(2)]
    for k in range(Z):
        for way, part in streams:
            total = term(k, way, part)
            if k > 0:
                copy(k - 1, way, part).wait_recv()
                total = total + inbox[k - 1, way, part].astype(jnp.float32)
            if k < Z - 1:
                outbox[k, way, part] = total.astype(jnp.bfloat16)
                if k == 0 and (way, part) == streams[0]:
                    pl.semaphore_wait(barrier, 2)
                copy(k, way, part).start()
            else:
                out[
                    part * half_rows : (part + 1) * half_rows,
                    way * half_cols : (way + 1) * half_cols,
                ] = total.astype(jnp.bfloat16)
    for k in range(Z - 1):
        for way, part in streams:
            copy(k, way, part).wait_send()


def project(hidden, weight):
    rows, cols = hidden.shape[0], weight.shape[0] // Z
    dma = pltpu.SemaphoreType.DMA
    vmem = pl.BlockSpec(memory_space=pltpu.VMEM)
    boxes = (Z - 1, 2, 2, rows // 2, cols // 2)
    return pl.pallas_call(
        project_kernel,
        out_shape=jax.ShapeDtypeStruct((rows, cols), jnp.bfloat16),
        in_specs=[vmem, vmem],
        out_specs=vmem,
        scratch_shapes=[
            pltpu.VMEM(boxes, jnp.bfloat16),
            pltpu.VMEM(boxes, jnp.bfloat16),
            dma((Z - 1, 2, 2)),
            dma((Z - 1, 2, 2)),
        ],
        compiler_params=pltpu.CompilerParams(
            collective_id=1, has_side_effects=True, vmem_limit_bytes=32 << 20
        ),
    )(hidden, weight)


def tables(heads):
    left = np.zeros((heads * FEAT, heads * PAD), np.float32)
    right = np.zeros((heads * FEAT, heads * PAD), np.float32)
    add_left = np.zeros((1, heads * PAD), np.float32)
    add_right = np.zeros((1, heads * PAD), np.float32)
    scale = np.zeros((1, heads * PAD), np.float32)
    twice = np.zeros((1, heads * PAD), np.float32)
    for h in range(heads):
        at = h * PAD
        add_left[0, at] = add_right[0, at] = scale[0, at] = twice[0, at] = 1.0
        for i in range(FEAT):
            at = h * PAD + 1 + i
            left[h * FEAT + i, at] = 1.0
            add_right[0, at] = scale[0, at] = twice[0, at] = 1.0
        at = h * PAD + 1 + FEAT
        for i in range(FEAT):
            for j in range(i, FEAT):
                left[h * FEAT + i, at] = 1.0
                right[h * FEAT + j, at] = 1.0
                scale[0, at] = np.float32(0.5**0.5)
                twice[0, at] = 1.0 if i == j else 2.0
                at += 1
    return left, right, add_left, add_right, scale, twice


def taylor(conv, heads):
    left, right, add_left, add_right, scale, twice = tables(heads)
    a = (conv.astype(jnp.float32) * FEAT ** (-0.25)).astype(jnp.bfloat16)
    one = jnp.dot(a, jnp.asarray(left, jnp.bfloat16), preferred_element_type=jnp.float32) + add_left
    two = jnp.dot(a, jnp.asarray(right, jnp.bfloat16), preferred_element_type=jnp.float32) + add_right
    return ((one * two) * scale).astype(jnp.bfloat16), jnp.asarray(twice, jnp.bfloat16)


def convolve(inputs, rim_rows, kernel, keep):
    padded = jnp.concatenate(
        [rim_rows.astype(jnp.float32) * keep, inputs.astype(jnp.float32)], axis=0
    )
    return (kernel[0] * padded[:-2] + kernel[1] * padded[1:-1] + kernel[2] * padded[2:]).astype(
        jnp.bfloat16
    )


def on_device(
    query_feat,
    key_feat,
    values,
    conv_query,
    conv_key,
    conv_value,
    norm_gain,
    out_weight,
    stream_ids,
):
    rows, qw = query_feat.shape
    heads = values.shape[1] // HD
    shards = lax.axis_size("seq")
    position = lax.axis_index("seq")
    own_stream = stream_ids[position]
    prior_stream = stream_ids[jnp.maximum(position - 1, 0)]
    keep = 1.0 - jnp.logical_or(position == 0, own_stream != prior_stream).astype(jnp.float32)
    rim = jnp.concatenate([query_feat[-2:], key_feat[-2:], values[-2:]], axis=1)
    rim = lax.ppermute(rim, "seq", [(i, i + 1) for i in range(shards - 1)])
    qconv = convolve(query_feat, rim[:, :qw], conv_query, keep)
    kconv = convolve(key_feat, rim[:, qw : 2 * qw], conv_key, keep)
    vconv = convolve(values, rim[:, 2 * qw :], conv_value, keep)
    phk, twice = taylor(kconv, heads)
    kv = [
        lax.dot_general(
            phk[:, h * PAD : (h + 1) * PAD],
            vconv[:, h * HD : (h + 1) * HD],
            (((0,), (0,)), ((), ())),
            preferred_element_type=jnp.float32,
        )
        for h in range(heads)
    ]
    pieces = jnp.concatenate(kv, axis=0).astype(jnp.bfloat16).reshape(-1, TILE, HD)
    weight, state = exchange(stream_ids, pieces, out_weight.T)
    weight = weight.reshape(-1, weight.shape[-1])
    state = state.reshape(heads, PAD, HD)
    phq, _ = taylor(qconv, heads)
    phq = phq * twice
    causal = jnp.tril(jnp.ones((rows, rows), jnp.bool_))
    hidden = []
    for h in range(heads):
        q = phq[:, h * PAD : (h + 1) * PAD]
        k = phk[:, h * PAD : (h + 1) * PAD]
        v = vconv[:, h * HD : (h + 1) * HD]
        scores = lax.dot_general(
            q, k, (((1,), (1,)), ((), ())), preferred_element_type=jnp.float32
        )
        scores = jnp.where(causal, scores, 0.0).astype(jnp.bfloat16)
        y = jnp.dot(scores, v, preferred_element_type=jnp.float32) + jnp.dot(
            q, state[h], preferred_element_type=jnp.float32
        )
        gain = norm_gain[h * HD : (h + 1) * HD]
        y = y * lax.rsqrt(jnp.mean(y * y, axis=-1, keepdims=True) + 1e-05) * gain
        hidden.append(y.astype(jnp.bfloat16))
    hidden = jnp.concatenate(hidden, axis=1)
    return project(hidden, weight)


def solution(mesh):
    placed = (
        P("seq", "head"),
        P("seq", "head"),
        P("seq", "head"),
        P(None, "head"),
        P(None, "head"),
        P(None, "head"),
        P("head"),
        P("head", "seq"),
        P(),
    )
    return jax.shard_map(
        on_device, mesh=mesh, in_specs=placed, out_specs=P("seq", "head"), check_vma=False
    )
```

```python
import numpy as np
import jax
import jax.numpy as jnp
from jax import lax
from jax.experimental import pallas as pl
from jax.experimental.pallas import tpu as pltpu
from jax.sharding import PartitionSpec as P

HD = 128
FEAT = 16
PAD = 160
X, Y, C = 4, 8, 2
SHARDS = X * Y * C
Z = 8
TILE = 16
MESH = pl.DeviceIdType.MESH


def remote(src, dst, send_sem, recv_sem, axis, target):
    return pltpu.make_async_remote_copy(
        src_ref=src,
        dst_ref=dst,
        send_sem=send_sem,
        recv_sem=recv_sem,
        device_id={axis: target},
        device_id_type=MESH,
    )


def shifted(x, rim, axis):
    where = lax.broadcasted_iota(jnp.int32, x.shape, axis)
    far, near = lax.slice_in_dim(rim, 0, 1, axis=axis), lax.slice_in_dim(rim, 1, 2, axis=axis)
    one = jnp.where(where == 0, near, pltpu.roll(x, 1, axis))
    two = jnp.where(where == 0, far, jnp.where(where == 1, near, pltpu.roll(x, 2, axis)))
    return one, two


def exchange_kernel(
    ids,
    q_in,
    k_in,
    v_in,
    cq,
    ck,
    cv,
    gain,
    w_ref,
    q_left,
    q_right,
    q_scale,
    k_left,
    k_right,
    k_scale,
    wout,
    hidden,
    q_rim,
    k_rim,
    v_rim,
    phk,
    phq,
    vconv,
    local,
    pieces,
    state,
    inbox,
    sums,
    rim_send,
    rim_recv,
    own_sem,
    x_send,
    x_recv,
    y_send,
    y_recv,
    c_send,
    c_recv,
    one_send,
    one_recv,
    two_send,
    two_recv,
    local_sem,
):
    npieces = pieces.shape[0]
    heads = phq.shape[0]
    rows = v_in.shape[0]
    per_head = npieces // heads
    me = lax.axis_index("seq")
    c = lax.rem(me, C)
    y = lax.rem(me // C, Y)
    x = me // (C * Y)

    def at(xx, yy, cc):
        return (lax.rem(xx + X, X) * Y + lax.rem(yy + Y, Y)) * C + cc

    barrier = pltpu.get_barrier_semaphore()

    @pl.loop(1, SHARDS)
    def _(j):
        pl.semaphore_signal(
            barrier, inc=1, device_id={"seq": lax.rem(me + j, SHARDS)}, device_id_type=MESH
        )

    own = pltpu.make_async_copy(w_ref, wout.at[x, y, c], own_sem)
    own.start()
    pl.semaphore_wait(barrier, SHARDS - 1)

    after = lax.rem(me + 1, SHARDS)
    edges = (
        (q_in.at[:, pl.ds(rows - 128, 128)], q_rim),
        (k_in.at[:, pl.ds(rows - 128, 128)], k_rim),
        (v_in.at[pl.ds(rows - TILE, TILE), :], v_rim),
    )
    rims = [
        remote(src, dst, rim_send.at[i], rim_recv.at[i], "seq", after)
        for i, (src, dst) in enumerate(edges)
    ]
    for copy in rims:
        copy.start()
    along_x = [
        remote(w_ref, wout.at[x, y, c], x_send.at[k], x_recv.at[k], "seq", at(x + k + 1, y, c))
        for k in range(X - 1)
    ]
    for copy in along_x:
        copy.start()

    handler = me < npieces

    def group(yy, part=None):
        yy = lax.rem(yy + Y, Y)
        if part is None:
            return wout.at[:, yy, c]
        return wout.at[part * (X // 2) : (part + 1) * (X // 2), yy, c]

    def hop(k, way, part):
        ref = group(y - k if way == 0 else y + k, part)
        return remote(
            ref,
            ref,
            y_send.at[way, k, part],
            y_recv.at[way, k, part],
            "seq",
            at(x, y + 1 if way == 0 else y - 1, c),
        )

    hops = []

    def launch(k):
        for part in range(2):
            for way in range(2):
                if k > 0:
                    hop(k - 1, way, part).wait_recv()
                if k < 3 or way == part:
                    hops.append(hop(k, way, part))
                    hops[-1].start()

    def across(j, yy):
        ref = group(yy)
        return remote(ref, ref, c_send.at[j], c_recv.at[j], "seq", at(x, y, 1 - c))

    keep = jnp.where((me > 0) & (ids[me] == ids[jnp.maximum(me - 1, 0)]), 1.0, 0.0)
    wide_ones = jnp.ones((TILE, rows), jnp.bfloat16)

    def features_in(src, rim, taps, axis_keep):
        past = rim[...].astype(jnp.float32)[:, 126:128] * axis_keep
        now = src[...].astype(jnp.float32)
        one, two = shifted(now, past, 1)
        conv = taps[:, 0:1] * two + taps[:, 1:2] * one + taps[:, 2:3] * now
        conv = conv.astype(jnp.bfloat16).astype(jnp.float32)
        return jnp.concatenate([(conv * FEAT ** (-0.25)).astype(jnp.bfloat16), wide_ones], axis=0)

    own.wait()
    for copy in rims:
        copy.wait_recv()
    k_a = features_in(k_in, k_rim, ck, keep)
    for h in range(heads):
        span = slice(h * PAD, (h + 1) * PAD)
        one = jnp.dot(k_left[span, :], k_a, preferred_element_type=jnp.float32)
        two = jnp.dot(k_right[span, :], k_a, preferred_element_type=jnp.float32)
        phk[h] = ((one * two) * k_scale[span, :]).astype(jnp.bfloat16)
        lanes = slice(h * HD, (h + 1) * HD)
        now = v_in[:, lanes].astype(jnp.float32)
        past = v_rim[:, lanes].astype(jnp.float32)[TILE - 2 : TILE, :] * keep
        one, two = shifted(now, past, 0)
        conv = cv[0:1, lanes] * two + cv[1:2, lanes] * one + cv[2:3, lanes] * now
        vconv[:, lanes] = conv.astype(jnp.bfloat16)
        kv = jnp.dot(phk[h], vconv[:, lanes], preferred_element_type=jnp.float32)
        pieces[h * per_head : (h + 1) * per_head] = kv.astype(jnp.bfloat16).reshape(
            per_head, TILE, HD
        )

    @pl.loop(0, npieces)
    def _(p):
        @pl.when(p != me)
        def _():
            remote(pieces.at[p], inbox.at[me], one_send, one_recv, "seq", p).start()

    @pl.when(handler)
    def _():
        mine = pltpu.make_async_copy(pieces.at[me], inbox.at[me], local_sem)
        mine.start()
        mine.wait()

    for copy in along_x:
        copy.wait_recv()
    launch(0)
    partner = [across(0, y)]
    partner[0].start()

    q_a = features_in(q_in, q_rim, cq, keep)

    def attend(h):
        turn = (((0,), (0,)), ((), ()))
        one = lax.dot_general(q_a, q_left[h], turn, preferred_element_type=jnp.float32)
        two = lax.dot_general(q_a, q_right[h], turn, preferred_element_type=jnp.float32)
        phq[h] = ((one * two) * q_scale[...]).astype(jnp.bfloat16)
        scores = jnp.dot(phq[h], phk[h], preferred_element_type=jnp.float32)
        i = lax.broadcasted_iota(jnp.int32, scores.shape, 0)
        j = lax.broadcasted_iota(jnp.int32, scores.shape, 1)
        scores = jnp.where(j <= i, scores, 0.0).astype(jnp.bfloat16)
        lanes = slice(h * HD, (h + 1) * HD)
        local[:, lanes] = jnp.dot(scores, vconv[:, lanes], preferred_element_type=jnp.float32)

    def relay(k):
        launch(k + 1)
        for j, yy in ((1 + 2 * k, y - 1 - k), (2 + 2 * k, y + 1 + k)):
            partner.append(across(j, yy))
            partner[-1].start()

    attend(0)
    attend(1)

    @pl.when(handler)
    def _():
        pltpu.make_async_copy(
            inbox.at[pl.ds(0, SHARDS - 1)], inbox.at[pl.ds(0, SHARDS - 1)], one_recv
        ).wait()

        def step(s, acc):
            before = jnp.maximum(s - 1, 0)
            same = jnp.where((s > 0) & (ids[s] == ids[before]), 1.0, 0.0)
            acc = (acc + inbox[before].astype(jnp.float32)) * same
            sums[s] = acc.astype(jnp.bfloat16)
            return acc

        lax.fori_loop(0, SHARDS, step, jnp.zeros(inbox.shape[1:], jnp.float32))

        @pl.loop(0, SHARDS)
        def _(s):
            @pl.when(s != me)
            def _():
                remote(sums.at[s], state.at[me], two_send, two_recv, "seq", s).start()

        mine = pltpu.make_async_copy(sums.at[me], state.at[me], local_sem)
        mine.start()
        mine.wait()

    relay(0)
    attend(2)
    attend(3)
    relay(1)

    def drain(count, sem):
        pltpu.make_async_copy(
            inbox.at[pl.ds(0, count)], inbox.at[pl.ds(0, count)], sem
        ).wait()

    @pl.when(handler)
    def _():
        drain(npieces - 1, two_recv)
        drain(SHARDS - 1, two_send)
        drain(npieces - 1, one_send)

    @pl.when(jnp.logical_not(handler))
    def _():
        drain(npieces, two_recv)
        drain(npieces, one_send)

    for h in range(heads):
        lanes = slice(h * HD, (h + 1) * HD)
        mine = state[h * per_head : (h + 1) * per_head].reshape(PAD, HD)
        total = local[:, lanes] + jnp.dot(phq[h], mine, preferred_element_type=jnp.float32)
        power = jnp.mean(total * total, axis=-1, keepdims=True)
        hidden[:, lanes] = (total * lax.rsqrt(power + 1e-05) * gain[:, lanes]).astype(jnp.bfloat16)

    relay(2)
    hop(3, 0, 0).wait_recv()
    hop(3, 1, 1).wait_recv()
    partner.append(across(7, y + 4))
    partner[-1].start()

    for copy in rims + along_x + hops:
        copy.wait_send()
    for copy in partner:
        copy.wait()


def exchange(ids, q, k, v, cq, ck, cv, gain, block, *constants):
    dma = pltpu.SemaphoreType.DMA
    vmem = pl.BlockSpec(memory_space=pltpu.VMEM)
    rows, wide = v.shape
    heads = wide // HD
    narrow = q.shape[0]
    npieces = heads * PAD // TILE
    half = jnp.bfloat16
    return pl.pallas_call(
        exchange_kernel,
        out_shape=(
            jax.ShapeDtypeStruct((X, Y, C) + block.shape, block.dtype),
            jax.ShapeDtypeStruct(v.shape, half),
        ),
        in_specs=[pl.BlockSpec(memory_space=pltpu.SMEM)] + [vmem] * (8 + len(constants)),
        out_specs=(vmem, vmem),
        scratch_shapes=[
            pltpu.VMEM((narrow, 128), half),
            pltpu.VMEM((narrow, 128), half),
            pltpu.VMEM((TILE, wide), half),
            pltpu.VMEM((heads, PAD, rows), half),
            pltpu.VMEM((heads, rows, PAD), half),
            pltpu.VMEM((rows, wide), half),
            pltpu.VMEM((rows, wide), jnp.float32),
            pltpu.VMEM((npieces, TILE, HD), half),
            pltpu.VMEM((npieces, TILE, HD), half),
            pltpu.VMEM((SHARDS, TILE, HD), half),
            pltpu.VMEM((SHARDS, TILE, HD), half),
            dma((3,)),
            dma((3,)),
            dma,
            dma((X - 1,)),
            dma((X - 1,)),
            dma((2, 4, 2)),
            dma((2, 4, 2)),
            dma((Y,)),
            dma((Y,)),
            dma,
            dma,
            dma,
            dma,
            dma,
        ],
        compiler_params=pltpu.CompilerParams(
            collective_id=0, has_side_effects=True, vmem_limit_bytes=40 << 20
        ),
    )(ids, q, k, v, cq, ck, cv, gain, block, *constants)


def project_kernel(hidden, weight, out, outbox, inbox, send, recv):
    z = lax.axis_index("head")
    up, down = lax.rem(z + 1, Z), lax.rem(z + Z - 1, Z)
    barrier = pltpu.get_barrier_semaphore()
    for neighbour in (up, down):
        pl.semaphore_signal(barrier, inc=1, device_id={"head": neighbour}, device_id_type=MESH)
    rows, cols = out.shape
    half_rows, half_cols = rows // 2, cols // 2

    def term(k, way, part):
        goal = lax.rem(z + 2 * Z - 1 - k, Z) if way == 0 else lax.rem(z + 1 + k, Z)
        first = pl.multiple_of(goal * cols + way * half_cols, half_cols)
        return lax.dot_general(
            hidden[part * half_rows : (part + 1) * half_rows, :],
            weight[pl.ds(first, half_cols), :],
            (((1,), (1,)), ((), ())),
            preferred_element_type=jnp.float32,
        )

    def copy(k, way, part):
        return remote(
            outbox.at[k, way, part],
            inbox.at[k, way, part],
            send.at[k, way, part],
            recv.at[k, way, part],
            "head",
            up if way == 0 else down,
        )

    streams = [(way, part) for part in range(2) for way in range(2)]
    for k in range(Z):
        for way, part in streams:
            total = term(k, way, part)
            if k > 0:
                copy(k - 1, way, part).wait_recv()
                total = total + inbox[k - 1, way, part].astype(jnp.float32)
            if k < Z - 1:
                outbox[k, way, part] = total.astype(jnp.bfloat16)
                if k == 0 and (way, part) == streams[0]:
                    pl.semaphore_wait(barrier, 2)
                copy(k, way, part).start()
            else:
                out[
                    part * half_rows : (part + 1) * half_rows,
                    way * half_cols : (way + 1) * half_cols,
                ] = total.astype(jnp.bfloat16)
    for k in range(Z - 1):
        for way, part in streams:
            copy(k, way, part).wait_send()


def project(hidden, weight):
    rows, cols = hidden.shape[0], weight.shape[0] // Z
    dma = pltpu.SemaphoreType.DMA
    vmem = pl.BlockSpec(memory_space=pltpu.VMEM)
    boxes = (Z - 1, 2, 2, rows // 2, cols // 2)
    return pl.pallas_call(
        project_kernel,
        out_shape=jax.ShapeDtypeStruct((rows, cols), jnp.bfloat16),
        in_specs=[vmem, vmem],
        out_specs=vmem,
        scratch_shapes=[
            pltpu.VMEM(boxes, jnp.bfloat16),
            pltpu.VMEM(boxes, jnp.bfloat16),
            dma((Z - 1, 2, 2)),
            dma((Z - 1, 2, 2)),
        ],
        compiler_params=pltpu.CompilerParams(
            collective_id=1, has_side_effects=True, vmem_limit_bytes=32 << 20
        ),
    )(hidden, weight)


def tables(heads):
    wide = heads * FEAT + TILE
    bias = heads * FEAT
    left = np.zeros((heads, PAD, wide), np.float32)
    right = np.zeros((heads, PAD, wide), np.float32)
    scale = np.zeros((PAD,), np.float32)
    twice = np.ones((PAD,), np.float32)
    scale[: 1 + FEAT] = 1.0
    left[:, 0, bias] = 1.0
    right[:, : 1 + FEAT, bias] = 1.0
    for h in range(heads):
        at = 1 + FEAT
        for i in range(FEAT):
            left[h, 1 + i, h * FEAT + i] = 1.0
            for j in range(i, FEAT):
                left[h, at, h * FEAT + i] = 1.0
                right[h, at, h * FEAT + j] = 1.0
                scale[at] = np.float32(0.5**0.5)
                twice[at] = 1.0 if i == j else 2.0
                at += 1
    flat = (heads * PAD, wide)
    return (
        jnp.asarray(left.transpose(0, 2, 1), jnp.bfloat16),
        jnp.asarray(right.transpose(0, 2, 1), jnp.bfloat16),
        jnp.asarray((scale * twice)[None, :]),
        jnp.asarray(left.reshape(flat), jnp.bfloat16),
        jnp.asarray(right.reshape(flat), jnp.bfloat16),
        jnp.asarray(np.tile(scale, heads)[:, None]),
    )


def on_device(
    query_feat,
    key_feat,
    values,
    conv_query,
    conv_key,
    conv_value,
    norm_gain,
    out_weight,
    stream_ids,
):
    heads = values.shape[1] // HD
    weight, hidden = exchange(
        stream_ids,
        query_feat.T,
        key_feat.T,
        values,
        conv_query.T,
        conv_key.T,
        conv_value,
        norm_gain[None, :],
        out_weight.T,
        *tables(heads),
    )
    return project(hidden, weight.reshape(-1, weight.shape[-1]))


def solution(mesh):
    placed = (
        P("seq", "head"),
        P("seq", "head"),
        P("seq", "head"),
        P(None, "head"),
        P(None, "head"),
        P(None, "head"),
        P("head"),
        P("head", "seq"),
        P(),
    )
    return jax.shard_map(
        on_device, mesh=mesh, in_specs=placed, out_specs=P("seq", "head"), check_vma=False
    )
```

```python
import numpy as np
import jax
import jax.numpy as jnp
from jax import lax
from jax.experimental import pallas as pl
from jax.experimental.pallas import tpu as pltpu
from jax.sharding import PartitionSpec as P

HD = 128
FEAT = 16
PAD = 160
X, Y, C = 4, 8, 2
SHARDS = X * Y * C
Z = 8
TILE = 16
NSCRATCH = 36
MESH = pl.DeviceIdType.MESH


def remote(src, dst, send_sem, recv_sem, axis, target):
    return pltpu.make_async_remote_copy(
        src_ref=src,
        dst_ref=dst,
        send_sem=send_sem,
        recv_sem=recv_sem,
        device_id={axis: target},
        device_id_type=MESH,
    )


def shifted(x, rim, axis):
    where = lax.broadcasted_iota(jnp.int32, x.shape, axis)
    far, near = lax.slice_in_dim(rim, 0, 1, axis=axis), lax.slice_in_dim(rim, 1, 2, axis=axis)
    one = jnp.where(where == 0, near, pltpu.roll(x, 1, axis))
    two = jnp.where(where == 0, far, jnp.where(where == 1, near, pltpu.roll(x, 2, axis)))
    return one, two


def layer_kernel(
    ids,
    *refs,
):
    count = (len(refs) - NSCRATCH) // 2
    w_ref, far, out = refs[0], refs[1:count], refs[count]
    near = refs[count + 1 : 2 * count]
    scratch = refs[2 * count :]
    mix_body(ids, w_ref, far, near, *scratch[:-4])
    project_body(scratch[1], scratch[0], out, *scratch[-4:])


def mix_body(
    ids,
    w_ref,
    far,
    near,
    wout,
    hidden,
    in_sem,
    q_rim,
    k_rim,
    v_rim,
    phk,
    phq,
    vconv,
    local,
    pieces,
    state,
    inbox,
    sums,
    rim_send,
    rim_recv,
    own_sem,
    x_send,
    x_recv,
    y_send,
    y_recv,
    b_send,
    b_recv,
    bx_send,
    bx_recv,
    c_send,
    c_recv,
    one_send,
    one_recv,
    two_send,
    two_recv,
    local_sem,
):
    fetches = [pltpu.make_async_copy(a, b, in_sem.at[i]) for i, (a, b) in enumerate(zip(far, near))]
    for copy in fetches:
        copy.start()
    (q_in, k_in, v_in, cq, ck, cv, gain) = near[:7]
    (q_left, q_right, q_scale, k_left, k_right, k_scale) = near[7:]
    npieces = pieces.shape[0]
    heads = phq.shape[0]
    rows = v_in.shape[0]
    per_head = npieces // heads
    me = lax.axis_index("seq")
    c = lax.rem(me, C)
    y = lax.rem(me // C, Y)
    x = me // (C * Y)

    def at(xx, yy, cc):
        return (lax.rem(xx + X, X) * Y + lax.rem(yy + Y, Y)) * C + cc

    barrier = pltpu.get_barrier_semaphore()

    @pl.loop(1, SHARDS)
    def _(j):
        pl.semaphore_signal(
            barrier, inc=1, device_id={"seq": lax.rem(me + j, SHARDS)}, device_id_type=MESH
        )

    z = lax.axis_index("head")
    for neighbour in (lax.rem(z + 1, Z), lax.rem(z + Z - 1, Z)):
        pl.semaphore_signal(barrier, inc=1, device_id={"head": neighbour}, device_id_type=MESH)
    own = pltpu.make_async_copy(w_ref, wout.at[x, y, c], own_sem)
    own.start()
    pl.semaphore_wait(barrier, SHARDS + 1)

    after = lax.rem(me + 1, SHARDS)
    edges = (
        (q_in.at[:, pl.ds(rows - 128, 128)], q_rim),
        (k_in.at[:, pl.ds(rows - 128, 128)], k_rim),
        (v_in.at[pl.ds(rows - TILE, TILE), :], v_rim),
    )
    rims = [
        remote(src, dst, rim_send.at[i], rim_recv.at[i], "seq", after)
        for i, (src, dst) in enumerate(edges)
    ]
    for copy in fetches[:3]:
        copy.wait()
    for copy in rims:
        copy.start()
    half = wout.shape[3] // 2
    top, low = pl.ds(0, half), pl.ds(half, half)
    own.wait()

    def spread(k, ref, send, recv, target):
        return remote(ref, ref, send.at[k], recv.at[k], "seq", target)

    along_x = [
        spread(k, wout.at[x, y, c, top], x_send, x_recv, at(x + k + 1, y, c)) for k in range(X - 1)
    ]
    along_y = [
        spread(k, wout.at[x, y, c, low], b_send, b_recv, at(x, y + k + 1, c)) for k in range(Y - 1)
    ]
    for copy in along_x + along_y:
        copy.start()

    handler = me < npieces

    def group(yy, part=None):
        yy = lax.rem(yy + Y, Y)
        if part is None:
            return wout.at[:, yy, c, top]
        return wout.at[part * (X // 2) : (part + 1) * (X // 2), yy, c, top]

    def column(xx, part=None):
        xx = lax.rem(xx + X, X)
        if part is None:
            return wout.at[xx, :, c, low]
        return wout.at[xx, part * (Y // 2) : (part + 1) * (Y // 2), c, low]

    def hop(k, way):
        ref = group(y - k if way == 0 else y + k, None if k < 3 else way)
        goal = at(x, y + 1 if way == 0 else y - 1, c)
        return remote(ref, ref, y_send.at[way, k], y_recv.at[way, k], "seq", goal)

    def leap(k, way):
        ref = column(x - k if way == 0 else x + k, None if k < 1 else way)
        goal = at(x + 1 if way == 0 else x - 1, y, c)
        return remote(ref, ref, bx_send.at[way, k], bx_recv.at[way, k], "seq", goal)

    hops = []
    partner = []

    def launch(kind, k):
        for way in range(2):
            if k > 0:
                kind(k - 1, way).wait_recv()
        for way in range(2):
            hops.append(kind(k, way))
            hops[-1].start()

    def across(j, ref):
        partner.append(remote(ref, ref, c_send.at[j], c_recv.at[j], "seq", at(x, y, 1 - c)))
        partner[-1].start()

    def relay(k):
        launch(hop, k + 1)
        across(1 + 2 * k, group(y - 1 - k))
        across(2 + 2 * k, group(y + 1 + k))

    keep = jnp.where((me > 0) & (ids[me] == ids[jnp.maximum(me - 1, 0)]), 1.0, 0.0)
    wide_ones = jnp.ones((TILE, rows), jnp.bfloat16)

    def features_in(src, rim, taps, axis_keep):
        past = rim[...].astype(jnp.float32)[:, 126:128] * axis_keep
        now = src[...].astype(jnp.float32)
        one, two = shifted(now, past, 1)
        conv = taps[:, 0:1] * two + taps[:, 1:2] * one + taps[:, 2:3] * now
        conv = conv.astype(jnp.bfloat16).astype(jnp.float32)
        return jnp.concatenate([(conv * FEAT ** (-0.25)).astype(jnp.bfloat16), wide_ones], axis=0)

    for copy in fetches[3:]:
        copy.wait()
    for copy in rims:
        copy.wait_recv()
    k_a = features_in(k_in, k_rim, ck, keep)
    for h in range(heads):
        span = slice(h * PAD, (h + 1) * PAD)
        one = jnp.dot(k_left[span, :], k_a, preferred_element_type=jnp.float32)
        two = jnp.dot(k_right[span, :], k_a, preferred_element_type=jnp.float32)
        phk[h] = ((one * two) * k_scale[span, :]).astype(jnp.bfloat16)
        lanes = slice(h * HD, (h + 1) * HD)
        now = v_in[:, lanes].astype(jnp.float32)
        past = v_rim[:, lanes].astype(jnp.float32)[TILE - 2 : TILE, :] * keep
        one, two = shifted(now, past, 0)
        conv = cv[0:1, lanes] * two + cv[1:2, lanes] * one + cv[2:3, lanes] * now
        vconv[:, lanes] = conv.astype(jnp.bfloat16)
        kv = jnp.dot(phk[h], vconv[:, lanes], preferred_element_type=jnp.float32)
        pieces[h * per_head : (h + 1) * per_head] = kv.astype(jnp.bfloat16).reshape(
            per_head, TILE, HD
        )
        if h == heads // 2 - 1:
            for copy in along_x:
                copy.wait_recv()
            launch(hop, 0)
            across(0, group(y))

    @pl.loop(0, npieces)
    def _(p):
        @pl.when(p != me)
        def _():
            remote(pieces.at[p], inbox.at[me], one_send, one_recv, "seq", p).start()

    @pl.when(handler)
    def _():
        mine = pltpu.make_async_copy(pieces.at[me], inbox.at[me], local_sem)
        mine.start()
        mine.wait()

    for copy in along_y:
        copy.wait_recv()
    launch(leap, 0)
    across(8, column(x))

    q_a = features_in(q_in, q_rim, cq, keep)

    def attend(h):
        turn = (((0,), (0,)), ((), ()))
        one = lax.dot_general(q_a, q_left[h], turn, preferred_element_type=jnp.float32)
        two = lax.dot_general(q_a, q_right[h], turn, preferred_element_type=jnp.float32)
        phq[h] = ((one * two) * q_scale[...]).astype(jnp.bfloat16)
        scores = jnp.dot(phq[h], phk[h], preferred_element_type=jnp.float32)
        i = lax.broadcasted_iota(jnp.int32, scores.shape, 0)
        j = lax.broadcasted_iota(jnp.int32, scores.shape, 1)
        scores = jnp.where(j <= i, scores, 0.0).astype(jnp.bfloat16)
        lanes = slice(h * HD, (h + 1) * HD)
        local[:, lanes] = jnp.dot(scores, vconv[:, lanes], preferred_element_type=jnp.float32)

    attend(0)
    relay(0)
    attend(1)

    @pl.when(handler)
    def _():
        pltpu.make_async_copy(
            inbox.at[pl.ds(0, SHARDS - 1)], inbox.at[pl.ds(0, SHARDS - 1)], one_recv
        ).wait()

        def step(s, acc):
            before = jnp.maximum(s - 1, 0)
            same = jnp.where((s > 0) & (ids[s] == ids[before]), 1.0, 0.0)
            acc = (acc + inbox[before].astype(jnp.float32)) * same
            sums[s] = acc.astype(jnp.bfloat16)
            return acc

        lax.fori_loop(0, SHARDS, step, jnp.zeros(inbox.shape[1:], jnp.float32))

        @pl.loop(0, SHARDS)
        def _(s):
            @pl.when(s != me)
            def _():
                remote(sums.at[s], state.at[me], two_send, two_recv, "seq", s).start()

        mine = pltpu.make_async_copy(sums.at[me], state.at[me], local_sem)
        mine.start()
        mine.wait()

    relay(1)
    launch(leap, 1)
    across(9, column(x - 1))
    across(10, column(x + 1))
    attend(2)
    relay(2)
    attend(3)
    leap(1, 0).wait_recv()
    leap(1, 1).wait_recv()
    across(11, column(x + 2))
    hop(3, 0).wait_recv()
    hop(3, 1).wait_recv()
    across(7, group(y + 4))

    def drain(count, sem):
        pltpu.make_async_copy(
            inbox.at[pl.ds(0, count)], inbox.at[pl.ds(0, count)], sem
        ).wait()

    @pl.when(handler)
    def _():
        drain(npieces - 1, two_recv)
        drain(SHARDS - 1, two_send)
        drain(npieces - 1, one_send)

    @pl.when(jnp.logical_not(handler))
    def _():
        drain(npieces, two_recv)
        drain(npieces, one_send)

    for h in range(heads):
        lanes = slice(h * HD, (h + 1) * HD)
        mine = state[h * per_head : (h + 1) * per_head].reshape(PAD, HD)
        total = local[:, lanes] + jnp.dot(phq[h], mine, preferred_element_type=jnp.float32)
        power = jnp.mean(total * total, axis=-1, keepdims=True)
        hidden[:, lanes] = (total * lax.rsqrt(power + 1e-05) * gain[:, lanes]).astype(jnp.bfloat16)

    for copy in rims + along_x + along_y + hops:
        copy.wait_send()
    for copy in partner:
        copy.wait()


def layer(ids, q, k, v, cq, ck, cv, gain, block, *constants):
    dma = pltpu.SemaphoreType.DMA
    vmem = pl.BlockSpec(memory_space=pltpu.VMEM)
    rows, wide = v.shape
    heads = wide // HD
    narrow = q.shape[0]
    npieces = heads * PAD // TILE
    half = jnp.bfloat16
    boxes = (Z - 1, 2, 2, rows // 2, SHARDS * block.shape[0] // Z // 2)
    inputs = (q, k, v, cq, ck, cv, gain) + constants
    return pl.pallas_call(
        layer_kernel,
        out_shape=jax.ShapeDtypeStruct((rows, SHARDS * block.shape[0] // Z), half),
        in_specs=[pl.BlockSpec(memory_space=pltpu.SMEM)]
        + [pl.BlockSpec(memory_space=pltpu.HBM)] * (1 + len(inputs)),
        out_specs=vmem,
        scratch_shapes=[pltpu.VMEM(a.shape, a.dtype) for a in inputs]
        + [
            pltpu.VMEM((X, Y, C) + block.shape, half),
            pltpu.VMEM(v.shape, half),
            dma((len(inputs),)),
            pltpu.VMEM((narrow, 128), half),
            pltpu.VMEM((narrow, 128), half),
            pltpu.VMEM((TILE, wide), half),
            pltpu.VMEM((heads, PAD, rows), half),
            pltpu.VMEM((heads, rows, PAD), half),
            pltpu.VMEM((rows, wide), half),
            pltpu.VMEM((rows, wide), jnp.float32),
            pltpu.VMEM((npieces, TILE, HD), half),
            pltpu.VMEM((npieces, TILE, HD), half),
            pltpu.VMEM((SHARDS, TILE, HD), half),
            pltpu.VMEM((SHARDS, TILE, HD), half),
            dma((3,)),
            dma((3,)),
            dma,
            dma((X - 1,)),
            dma((X - 1,)),
            dma((2, 4)),
            dma((2, 4)),
            dma((Y - 1,)),
            dma((Y - 1,)),
            dma((2, 2)),
            dma((2, 2)),
            dma((X + Y,)),
            dma((X + Y,)),
            dma,
            dma,
            dma,
            dma,
            dma,
            pltpu.VMEM(boxes, half),
            pltpu.VMEM(boxes, half),
            dma(boxes[:3]),
            dma(boxes[:3]),
        ],
        compiler_params=pltpu.CompilerParams(
            collective_id=0, has_side_effects=True, vmem_limit_bytes=60 << 20
        ),
    )(ids, block, *inputs)


def project_body(hidden, wout, out, outbox, inbox, send, recv):
    z = lax.axis_index("head")
    up, down = lax.rem(z + 1, Z), lax.rem(z + Z - 1, Z)
    rows, cols = out.shape
    half_rows, half_cols = rows // 2, cols // 2

    def term(k, way, part):
        goal = lax.rem(z + 2 * Z - 1 - k, Z) if way == 0 else lax.rem(z + 1 + k, Z)
        first = goal * (SHARDS // Z) + way * (SHARDS // Z // 2)
        weight = wout[first // (Y * C), pl.ds(lax.rem(first // C, Y), SHARDS // Z // 2 // C)]
        return lax.dot_general(
            hidden[part * half_rows : (part + 1) * half_rows, :],
            weight.reshape(half_cols, weight.shape[-1]),
            (((1,), (1,)), ((), ())),
            preferred_element_type=jnp.float32,
        )

    def copy(k, way, part):
        return remote(
            outbox.at[k, way, part],
            inbox.at[k, way, part],
            send.at[k, way, part],
            recv.at[k, way, part],
            "head",
            up if way == 0 else down,
        )

    streams = [(way, part) for part in range(2) for way in range(2)]
    for k in range(Z):
        for way, part in streams:
            total = term(k, way, part)
            if k > 0:
                copy(k - 1, way, part).wait_recv()
                total = total + inbox[k - 1, way, part].astype(jnp.float32)
            if k < Z - 1:
                outbox[k, way, part] = total.astype(jnp.bfloat16)
                copy(k, way, part).start()
            else:
                out[
                    part * half_rows : (part + 1) * half_rows,
                    way * half_cols : (way + 1) * half_cols,
                ] = total.astype(jnp.bfloat16)
    for k in range(Z - 1):
        for way, part in streams:
            copy(k, way, part).wait_send()


def tables(heads):
    wide = heads * FEAT + TILE
    bias = heads * FEAT
    left = np.zeros((heads, PAD, wide), np.float32)
    right = np.zeros((heads, PAD, wide), np.float32)
    scale = np.zeros((PAD,), np.float32)
    twice = np.ones((PAD,), np.float32)
    scale[: 1 + FEAT] = 1.0
    left[:, 0, bias] = 1.0
    right[:, : 1 + FEAT, bias] = 1.0
    for h in range(heads):
        at = 1 + FEAT
        for i in range(FEAT):
            left[h, 1 + i, h * FEAT + i] = 1.0
            for j in range(i, FEAT):
                left[h, at, h * FEAT + i] = 1.0
                right[h, at, h * FEAT + j] = 1.0
                scale[at] = np.float32(0.5**0.5)
                twice[at] = 1.0 if i == j else 2.0
                at += 1
    flat = (heads * PAD, wide)
    return (
        jnp.asarray(left.transpose(0, 2, 1), jnp.bfloat16),
        jnp.asarray(right.transpose(0, 2, 1), jnp.bfloat16),
        jnp.asarray((scale * twice)[None, :]),
        jnp.asarray(left.reshape(flat), jnp.bfloat16),
        jnp.asarray(right.reshape(flat), jnp.bfloat16),
        jnp.asarray(np.tile(scale, heads)[:, None]),
    )


def on_device(
    query_feat,
    key_feat,
    values,
    conv_query,
    conv_key,
    conv_value,
    norm_gain,
    out_weight,
    stream_ids,
):
    heads = values.shape[1] // HD
    return layer(
        stream_ids,
        query_feat.T,
        key_feat.T,
        values,
        conv_query.T,
        conv_key.T,
        conv_value,
        norm_gain[None, :],
        out_weight.T,
        *tables(heads),
    )


def solution(mesh):
    placed = (
        P("seq", "head"),
        P("seq", "head"),
        P("seq", "head"),
        P(None, "head"),
        P(None, "head"),
        P(None, "head"),
        P("head"),
        P("head", "seq"),
        P(),
    )
    return jax.shard_map(
        on_device, mesh=mesh, in_specs=placed, out_specs=P("seq", "head"), check_vma=False
    )
```

```python
import numpy as np
import jax
import jax.numpy as jnp
from jax import lax
from jax.experimental import pallas as pl
from jax.experimental.pallas import tpu as pltpu
from jax.sharding import PartitionSpec as P

HD = 128
FEAT = 16
PAD = 160
X, Y, C = 4, 8, 2
SHARDS = X * Y * C
Z = 8
TILE = 16
NSCRATCH = 36
MESH = pl.DeviceIdType.MESH


def remote(src, dst, send_sem, recv_sem, axis, target):
    return pltpu.make_async_remote_copy(
        src_ref=src,
        dst_ref=dst,
        send_sem=send_sem,
        recv_sem=recv_sem,
        device_id={axis: target},
        device_id_type=MESH,
    )


def shifted(x, rim, axis):
    where = lax.broadcasted_iota(jnp.int32, x.shape, axis)
    far, near = lax.slice_in_dim(rim, 0, 1, axis=axis), lax.slice_in_dim(rim, 1, 2, axis=axis)
    one = jnp.where(where == 0, near, pltpu.roll(x, 1, axis))
    two = jnp.where(where == 0, far, jnp.where(where == 1, near, pltpu.roll(x, 2, axis)))
    return one, two


def layer_kernel(
    ids,
    *refs,
):
    count = (len(refs) - NSCRATCH) // 2
    w_ref, far, out = refs[0], refs[1:count], refs[count]
    near = refs[count + 1 : 2 * count]
    scratch = refs[2 * count :]
    mix_body(ids, w_ref, far, near, *scratch[:-4])
    project_body(scratch[1], scratch[0], out, *scratch[-4:])


def mix_body(
    ids,
    w_ref,
    far,
    near,
    wout,
    hidden,
    in_sem,
    q_rim,
    k_rim,
    v_rim,
    phk,
    phq,
    vconv,
    local,
    pieces,
    state,
    inbox,
    sums,
    rim_send,
    rim_recv,
    own_sem,
    x_send,
    x_recv,
    y_send,
    y_recv,
    b_send,
    b_recv,
    bx_send,
    bx_recv,
    c_send,
    c_recv,
    one_send,
    one_recv,
    two_send,
    two_recv,
    local_sem,
):
    fetches = [pltpu.make_async_copy(a, b, in_sem.at[i]) for i, (a, b) in enumerate(zip(far, near))]
    for copy in fetches:
        copy.start()
    (q_in, k_in, v_in, cq, ck, cv, gain) = near[:7]
    (q_left, q_right, q_scale, k_left, k_right, k_scale) = near[7:]
    npieces = pieces.shape[0]
    heads = phq.shape[0]
    rows = v_in.shape[0]
    per_head = npieces // heads
    me = lax.axis_index("seq")
    c = lax.rem(me, C)
    y = lax.rem(me // C, Y)
    x = me // (C * Y)

    def at(xx, yy, cc):
        return (lax.rem(xx + X, X) * Y + lax.rem(yy + Y, Y)) * C + cc

    barrier = pltpu.get_barrier_semaphore()

    @pl.loop(1, SHARDS)
    def _(j):
        pl.semaphore_signal(
            barrier, inc=1, device_id={"seq": lax.rem(me + j, SHARDS)}, device_id_type=MESH
        )

    z = lax.axis_index("head")
    for neighbour in (lax.rem(z + 1, Z), lax.rem(z + Z - 1, Z)):
        pl.semaphore_signal(barrier, inc=1, device_id={"head": neighbour}, device_id_type=MESH)
    own = pltpu.make_async_copy(w_ref, wout.at[x, y, c], own_sem)
    own.start()
    pl.semaphore_wait(barrier, SHARDS + 1)

    after = lax.rem(me + 1, SHARDS)
    edges = (
        (q_in.at[:, pl.ds(rows - 128, 128)], q_rim),
        (k_in.at[:, pl.ds(rows - 128, 128)], k_rim),
        (v_in.at[pl.ds(rows - TILE, TILE), :], v_rim),
    )
    rims = [
        remote(src, dst, rim_send.at[i], rim_recv.at[i], "seq", after)
        for i, (src, dst) in enumerate(edges)
    ]
    for copy in fetches[:3]:
        copy.wait()
    for copy in rims:
        copy.start()
    half = wout.shape[3] // 2
    top, low = pl.ds(0, half), pl.ds(half, half)
    own.wait()

    def spread(k, ref, send, recv, target):
        return remote(ref, ref, send.at[k], recv.at[k], "seq", target)

    along_x = [
        spread(k, wout.at[x, y, c, top], x_send, x_recv, at(x + k + 1, y, c)) for k in range(X - 1)
    ]
    along_y = [
        spread(k, wout.at[x, y, c, low], b_send, b_recv, at(x, y + k + 1, c)) for k in range(Y - 1)
    ]
    for copy in along_x + along_y:
        copy.start()

    handler = me < npieces

    def group(yy, part=None):
        yy = lax.rem(yy + Y, Y)
        if part is None:
            return wout.at[:, yy, c, top]
        return wout.at[part * (X // 2) : (part + 1) * (X // 2), yy, c, top]

    def column(xx, part=None):
        xx = lax.rem(xx + X, X)
        if part is None:
            return wout.at[xx, :, c, low]
        return wout.at[xx, part * (Y // 2) : (part + 1) * (Y // 2), c, low]

    def hop(k, way):
        ref = group(y - k if way == 0 else y + k, None if k < 3 else way)
        goal = at(x, y + 1 if way == 0 else y - 1, c)
        return remote(ref, ref, y_send.at[way, k], y_recv.at[way, k], "seq", goal)

    def leap(k, way):
        ref = column(x - k if way == 0 else x + k, None if k < 1 else way)
        goal = at(x + 1 if way == 0 else x - 1, y, c)
        return remote(ref, ref, bx_send.at[way, k], bx_recv.at[way, k], "seq", goal)

    hops = []
    partner = []

    def launch(kind, k):
        for way in range(2):
            if k > 0:
                kind(k - 1, way).wait_recv()
        for way in range(2):
            hops.append(kind(k, way))
            hops[-1].start()

    def across(j, ref):
        partner.append(remote(ref, ref, c_send.at[j], c_recv.at[j], "seq", at(x, y, 1 - c)))
        partner[-1].start()

    def relay(k):
        launch(hop, k + 1)
        across(1 + 2 * k, group(y - 1 - k))
        across(2 + 2 * k, group(y + 1 + k))

    keep = jnp.where((me > 0) & (ids[me] == ids[jnp.maximum(me - 1, 0)]), 1.0, 0.0)
    wide_ones = jnp.ones((TILE, rows), jnp.bfloat16)

    def features_in(src, rim, taps, axis_keep):
        past = rim[...].astype(jnp.float32)[:, 126:128] * axis_keep
        now = src[...].astype(jnp.float32)
        one, two = shifted(now, past, 1)
        turned = jnp.transpose(taps[...])
        conv = turned[:, 0:1] * two + turned[:, 1:2] * one + turned[:, 2:3] * now
        conv = conv.astype(jnp.bfloat16).astype(jnp.float32)
        return jnp.concatenate([(conv * FEAT ** (-0.25)).astype(jnp.bfloat16), wide_ones], axis=0)

    for copy in fetches[3:]:
        copy.wait()
    for copy in rims:
        copy.wait_recv()
    k_a = features_in(k_in, k_rim, ck, keep)
    for h in range(heads):
        span = slice(h * PAD, (h + 1) * PAD)
        one = jnp.dot(k_left[span, :], k_a, preferred_element_type=jnp.float32)
        two = jnp.dot(k_right[span, :], k_a, preferred_element_type=jnp.float32)
        phk[h] = ((one * two) * k_scale[span, :]).astype(jnp.bfloat16)
        lanes = slice(h * HD, (h + 1) * HD)
        now = v_in[:, lanes].astype(jnp.float32)
        past = v_rim[:, lanes].astype(jnp.float32)[TILE - 2 : TILE, :] * keep
        one, two = shifted(now, past, 0)
        conv = cv[0:1, lanes] * two + cv[1:2, lanes] * one + cv[2:3, lanes] * now
        vconv[:, lanes] = conv.astype(jnp.bfloat16)
        kv = jnp.dot(phk[h], vconv[:, lanes], preferred_element_type=jnp.float32)
        pieces[h * per_head : (h + 1) * per_head] = kv.astype(jnp.bfloat16).reshape(
            per_head, TILE, HD
        )

    @pl.loop(0, npieces)
    def _(p):
        @pl.when(p != me)
        def _():
            remote(pieces.at[p], inbox.at[me], one_send, one_recv, "seq", p).start()

    @pl.when(handler)
    def _():
        mine = pltpu.make_async_copy(pieces.at[me], inbox.at[me], local_sem)
        mine.start()
        mine.wait()

    for copy in along_x:
        copy.wait_recv()
    launch(hop, 0)
    across(0, group(y))
    for copy in along_y:
        copy.wait_recv()
    launch(leap, 0)
    across(8, column(x))

    q_a = features_in(q_in, q_rim, cq, keep)

    def attend(h):
        turn = (((0,), (0,)), ((), ()))
        one = lax.dot_general(q_a, q_left[h], turn, preferred_element_type=jnp.float32)
        two = lax.dot_general(q_a, q_right[h], turn, preferred_element_type=jnp.float32)
        phq[h] = ((one * two) * q_scale[...]).astype(jnp.bfloat16)
        scores = jnp.dot(phq[h], phk[h], preferred_element_type=jnp.float32)
        i = lax.broadcasted_iota(jnp.int32, scores.shape, 0)
        j = lax.broadcasted_iota(jnp.int32, scores.shape, 1)
        scores = jnp.where(j <= i, scores, 0.0).astype(jnp.bfloat16)
        lanes = slice(h * HD, (h + 1) * HD)
        local[:, lanes] = jnp.dot(scores, vconv[:, lanes], preferred_element_type=jnp.float32)

    attend(0)
    relay(0)
    attend(1)

    @pl.when(handler)
    def _():
        pltpu.make_async_copy(
            inbox.at[pl.ds(0, SHARDS - 1)], inbox.at[pl.ds(0, SHARDS - 1)], one_recv
        ).wait()

        def step(s, acc):
            before = jnp.maximum(s - 1, 0)
            same = jnp.where((s > 0) & (ids[s] == ids[before]), 1.0, 0.0)
            acc = (acc + inbox[before].astype(jnp.float32)) * same
            sums[s] = acc.astype(jnp.bfloat16)
            return acc

        lax.fori_loop(0, SHARDS, step, jnp.zeros(inbox.shape[1:], jnp.float32))

        @pl.loop(0, SHARDS)
        def _(s):
            @pl.when(s != me)
            def _():
                remote(sums.at[s], state.at[me], two_send, two_recv, "seq", s).start()

        mine = pltpu.make_async_copy(sums.at[me], state.at[me], local_sem)
        mine.start()
        mine.wait()

    relay(1)
    launch(leap, 1)
    across(9, column(x - 1))
    across(10, column(x + 1))
    attend(2)
    relay(2)
    attend(3)
    leap(1, 0).wait_recv()
    leap(1, 1).wait_recv()
    across(11, column(x + 2))
    hop(3, 0).wait_recv()
    hop(3, 1).wait_recv()
    across(7, group(y + 4))

    def drain(count, sem):
        pltpu.make_async_copy(
            inbox.at[pl.ds(0, count)], inbox.at[pl.ds(0, count)], sem
        ).wait()

    @pl.when(handler)
    def _():
        drain(npieces - 1, two_recv)
        drain(SHARDS - 1, two_send)
        drain(npieces - 1, one_send)

    @pl.when(jnp.logical_not(handler))
    def _():
        drain(npieces, two_recv)
        drain(npieces, one_send)

    for h in range(heads):
        lanes = slice(h * HD, (h + 1) * HD)
        mine = state[h * per_head : (h + 1) * per_head].reshape(PAD, HD)
        total = local[:, lanes] + jnp.dot(phq[h], mine, preferred_element_type=jnp.float32)
        power = jnp.mean(total * total, axis=-1, keepdims=True)
        hidden[:, lanes] = (total * lax.rsqrt(power + 1e-05) * gain[:, lanes]).astype(jnp.bfloat16)

    for copy in rims + along_x + along_y + hops:
        copy.wait_send()
    for copy in partner:
        copy.wait()


def layer(ids, q, k, v, cq, ck, cv, gain, block, *constants):
    dma = pltpu.SemaphoreType.DMA
    vmem = pl.BlockSpec(memory_space=pltpu.VMEM)
    rows, wide = v.shape
    heads = wide // HD
    narrow = q.shape[0]
    npieces = heads * PAD // TILE
    half = jnp.bfloat16
    boxes = (Z - 1, 2, 2, rows // 2, SHARDS * block.shape[0] // Z // 2)
    inputs = (q, k, v, cq, ck, cv, gain) + constants
    return pl.pallas_call(
        layer_kernel,
        out_shape=jax.ShapeDtypeStruct((rows, SHARDS * block.shape[0] // Z), half),
        in_specs=[pl.BlockSpec(memory_space=pltpu.SMEM)]
        + [pl.BlockSpec(memory_space=pltpu.HBM)] * (1 + len(inputs)),
        out_specs=vmem,
        scratch_shapes=[pltpu.VMEM(a.shape, a.dtype) for a in inputs]
        + [
            pltpu.VMEM((X, Y, C) + block.shape, half),
            pltpu.VMEM(v.shape, half),
            dma((len(inputs),)),
            pltpu.VMEM((narrow, 128), half),
            pltpu.VMEM((narrow, 128), half),
            pltpu.VMEM((TILE, wide), half),
            pltpu.VMEM((heads, PAD, rows), half),
            pltpu.VMEM((heads, rows, PAD), half),
            pltpu.VMEM((rows, wide), half),
            pltpu.VMEM((rows, wide), jnp.float32),
            pltpu.VMEM((npieces, TILE, HD), half),
            pltpu.VMEM((npieces, TILE, HD), half),
            pltpu.VMEM((SHARDS, TILE, HD), half),
            pltpu.VMEM((SHARDS, TILE, HD), half),
            dma((3,)),
            dma((3,)),
            dma,
            dma((X - 1,)),
            dma((X - 1,)),
            dma((2, 4)),
            dma((2, 4)),
            dma((Y - 1,)),
            dma((Y - 1,)),
            dma((2, 2)),
            dma((2, 2)),
            dma((X + Y,)),
            dma((X + Y,)),
            dma,
            dma,
            dma,
            dma,
            dma,
            pltpu.VMEM(boxes, half),
            pltpu.VMEM(boxes, half),
            dma(boxes[:3]),
            dma(boxes[:3]),
        ],
        compiler_params=pltpu.CompilerParams(
            collective_id=0, has_side_effects=True, vmem_limit_bytes=60 << 20
        ),
    )(ids, block, *inputs)


def project_body(hidden, wout, out, outbox, inbox, send, recv):
    z = lax.axis_index("head")
    up, down = lax.rem(z + 1, Z), lax.rem(z + Z - 1, Z)
    rows, cols = out.shape
    half_rows, half_cols = rows // 2, cols // 2

    def term(k, way, part):
        goal = lax.rem(z + 2 * Z - 1 - k, Z) if way == 0 else lax.rem(z + 1 + k, Z)
        first = goal * (SHARDS // Z) + way * (SHARDS // Z // 2)
        weight = wout[first // (Y * C), pl.ds(lax.rem(first // C, Y), SHARDS // Z // 2 // C)]
        return lax.dot_general(
            hidden[part * half_rows : (part + 1) * half_rows, :],
            weight.reshape(half_cols, weight.shape[-1]),
            (((1,), (1,)), ((), ())),
            preferred_element_type=jnp.float32,
        )

    def copy(k, way, part):
        return remote(
            outbox.at[k, way, part],
            inbox.at[k, way, part],
            send.at[k, way, part],
            recv.at[k, way, part],
            "head",
            up if way == 0 else down,
        )

    streams = [(way, part) for part in range(2) for way in range(2)]
    for k in range(Z):
        for way, part in streams:
            total = term(k, way, part)
            if k > 0:
                copy(k - 1, way, part).wait_recv()
                total = total + inbox[k - 1, way, part].astype(jnp.float32)
            if k < Z - 1:
                outbox[k, way, part] = total.astype(jnp.bfloat16)
                copy(k, way, part).start()
            else:
                out[
                    part * half_rows : (part + 1) * half_rows,
                    way * half_cols : (way + 1) * half_cols,
                ] = total.astype(jnp.bfloat16)
    for k in range(Z - 1):
        for way, part in streams:
            copy(k, way, part).wait_send()


def tables(heads):
    wide = heads * FEAT + TILE
    bias = heads * FEAT
    left = np.zeros((heads, PAD, wide), np.float32)
    right = np.zeros((heads, PAD, wide), np.float32)
    scale = np.zeros((PAD,), np.float32)
    twice = np.ones((PAD,), np.float32)
    scale[: 1 + FEAT] = 1.0
    left[:, 0, bias] = 1.0
    right[:, : 1 + FEAT, bias] = 1.0
    for h in range(heads):
        at = 1 + FEAT
        for i in range(FEAT):
            left[h, 1 + i, h * FEAT + i] = 1.0
            for j in range(i, FEAT):
                left[h, at, h * FEAT + i] = 1.0
                right[h, at, h * FEAT + j] = 1.0
                scale[at] = np.float32(0.5**0.5)
                twice[at] = 1.0 if i == j else 2.0
                at += 1
    flat = (heads * PAD, wide)
    return (
        jnp.asarray(left.transpose(0, 2, 1), jnp.bfloat16),
        jnp.asarray(right.transpose(0, 2, 1), jnp.bfloat16),
        jnp.asarray((scale * twice)[None, :]),
        jnp.asarray(left.reshape(flat), jnp.bfloat16),
        jnp.asarray(right.reshape(flat), jnp.bfloat16),
        jnp.asarray(np.tile(scale, heads)[:, None]),
    )


def on_device(
    query_feat,
    key_feat,
    values,
    conv_query,
    conv_key,
    conv_value,
    norm_gain,
    out_weight,
    stream_ids,
):
    heads = values.shape[1] // HD
    return layer(
        stream_ids,
        query_feat.T,
        key_feat.T,
        values,
        conv_query,
        conv_key,
        conv_value,
        norm_gain[None, :],
        out_weight.T,
        *tables(heads),
    )


def solution(mesh):
    placed = (
        P("seq", "head"),
        P("seq", "head"),
        P("seq", "head"),
        P(None, "head"),
        P(None, "head"),
        P(None, "head"),
        P("head"),
        P("head", "seq"),
        P(),
    )
    return jax.shard_map(
        on_device, mesh=mesh, in_specs=placed, out_specs=P("seq", "head"), check_vma=False
    )
```
